32 devices in a mesh: expert: 8 (over z, x), width: 4 (over y, core).
Axes of the slice: x: 2, y: 2, z: 4, core: 2. Of those that a mesh axis runs over, the one named last changes fastest.
Arguments:
- tokens: bfloat16 [1024, 4096], P('expert'), may hold values from -6 to 6
- expert_ids: int32 [1024, 8], P('expert'), may hold values from 0 to 15, all different within a row; in each aligned block of 128 rows (0 to 127, 128 to 255, ...) at most 128 rows name the same one
- combine_weights: float32 [1024, 8], P('expert'), may hold values from 0.05 to 0.3
- gate_weight: bfloat16 [16, 4096, 1536], P('expert', None, 'width'), may hold values from -0.09375 to 0.09375
- up_weight: bfloat16 [16, 4096, 1536], P('expert', None, 'width'), may hold values from -0.09375 to 0.09375
- down_weight: bfloat16 [16, 1536, 4096], P('expert', 'width'), may hold values from -0.15625 to 0.15625
Outputs:
- mixed: bfloat16 [1024, 4096], P('expert', 'width')
The draws below stay inside these ranges and needn't reach their ends.
Inputs may be any that keep to these rules, and one draw needn't show every extreme that they name: `expert_ids`: each token names 8 different experts. Within the tokens of one index of expert (aligned blocks of 128 tokens) no expert is named by more than 128 tokens, a bound that some block reaches.
All inputs are finite; a program needn't handle non-finite values.
Results may differ from the reference program's by a relative error of at most 0.012.
Values may be sent and summed in bfloat16 or wider, within the bound.
A program may use at most 128 MiB of HBM per device.

```python
import math
import jax
import jax.numpy as jnp
import numpy as np
from jax import lax

D = 4096
FF = 1536
TOP = 8
TOK_DEV = 128
EXPERTS = 16
TOKENS = 1024
MOST = 128
N_EXPERT = 8
N_WIDTH = 4


def block_scale(key, extent, cuts, least, largest):
    loudness = 1.0
    for position, shards_of in cuts:
        steps = jax.random.uniform(jax.random.fold_in(jax.random.fold_in(key, 6), position), (shards_of,), jnp.float32, least / len(cuts), largest / len(cuts))
        loudness = loudness * jnp.repeat(jnp.exp(steps), extent[position] // shards_of).reshape((-1,) + (1,) * (len(extent) - 1 - position))
    return loudness


def deal_out(stream_key, own, number, rows, count, top, reach, slope):
    ranking = jax.random.permutation(stream_key, count)
    crowded, common = shares(count, rows * top, reach, slope, True), shares(count, rows * top, reach, slope, False)
    places = jnp.arange(count)

    def named(sizes, offset_by):
        used = int((sizes > 0).sum())
        fixed = max(1, used // 4)
        moved = fixed + (places - fixed + offset_by * (used - fixed)) % max(1, count - fixed)
        return jnp.zeros((count,), jnp.int32).at[ranking[jnp.where(places < fixed, places, moved)]].set(jnp.asarray(sizes, jnp.int32))

    sizes = jnp.where(number % 4 == 0, named(crowded, number // 4), named(common, number - number // 4 - 1))
    mixed = jax.random.permutation(jax.random.fold_in(own, 3), count)
    source_of, sink = mixed[0:count // 2 * 2:2], mixed[1:count // 2 * 2:2]
    room = jnp.minimum(sizes[source_of] - 1, reach - sizes[sink]) // 2
    room = jnp.where((source_of == ranking[0]) | (sink == ranking[0]) | (sizes[sink] == 0), 0, jnp.maximum(room, 0))
    moved = jax.random.randint(jax.random.fold_in(own, 4), (count // 2,), 0, 1 << 20) % (room + 1)
    sizes = sizes.at[source_of].add(-moved).at[sink].add(moved)
    members = jnp.searchsorted(jnp.cumsum(sizes), jnp.arange(rows * top), side="right").astype(jnp.int32)
    listing = members.reshape(top, rows).T
    listing = listing[jax.random.permutation(jax.random.fold_in(own, 1), rows)]
    offset_by = jax.random.randint(jax.random.fold_in(own, 2), (rows, 1), 0, top)
    return jnp.take_along_axis(listing, (jnp.arange(top)[None, :] + offset_by) % top, axis=1)


def shares(number_of, total, bound, skew, full):
    portions = [(1 << 20) // math.isqrt(grade ** skew) + 1 for grade in range(1, number_of + 1)]
    largest = bound if full else min(bound, max(-(-total // number_of), total * portions[0] // sum(portions)))
    least = 1 if total - largest >= number_of - 1 else 0
    given, spare = [largest] + [least] * (number_of - 1), total - largest - least * (number_of - 1)
    while spare > 0:
        movable = [i for i in range(1, number_of) if given[i] < largest] or [i for i in range(1, number_of) if given[i] < bound]
        pool, remaining = sum([portions[i] for i in movable]), spare
        for i in movable:
            addition = min(bound - given[i], max(1, remaining * portions[i] // pool), spare)
            given[i] = given[i] + addition
            spare = spare - addition
    return np.array(given)


def scatter_about(own_key, shape, deviation, limit, pieces=(), kind=jnp.bfloat16):
    result = jax.random.normal(own_key, shape, jnp.float32) * deviation
    if len(pieces) > 0:
        result = block_scale(own_key, shape, pieces, -0.22, 0.18) * result
    return jnp.clip(result, min=-limit, max=limit).astype(kind)


def setup_inputs(seed: int = 0) -> dict:
    key_list = jax.random.split(jax.random.key(seed), 7)
    tokens = scatter_about(key_list[0], (TOKENS, D), 1.0, 6.0, ((0, 8),))
    expert_ids_keys = jax.random.split(jax.random.fold_in(key_list[1], 1), TOKENS // TOK_DEV)
    expert_ids_turns = jax.random.permutation(jax.random.fold_in(key_list[1], 3), TOKENS // TOK_DEV)
    expert_ids = jax.vmap(lambda own, number: deal_out(jax.random.fold_in(key_list[1], 2), own, number, TOK_DEV, EXPERTS, TOP, MOST, 1))(expert_ids_keys, expert_ids_turns).reshape((TOKENS, TOP))
    combine_weights = jnp.clip(0.05 + 0.25 * jax.random.uniform(key_list[2], (TOKENS, TOP), jnp.float32) ** block_scale(key_list[2], (TOKENS, TOP), ((0, 8),), -0.2, 0.2), 0.05, 0.3)
    gate_weight = scatter_about(key_list[3], (EXPERTS, D, FF), D ** -0.5, 0.09375, ((0, 8), (2, 4)))
    up_weight = scatter_about(key_list[4], (EXPERTS, D, FF), D ** -0.5, 0.09375, ((0, 8), (2, 4)))
    down_weight = scatter_about(key_list[5], (EXPERTS, FF, D), FF ** -0.5, 0.15625, ((0, 8), (1, 4)))
    return dict(tokens=tokens, expert_ids=expert_ids, combine_weights=combine_weights, gate_weight=gate_weight, up_weight=up_weight, down_weight=down_weight)


def ranks_of(expert_ids):
    flat_ids = expert_ids.reshape(N_EXPERT, TOK_DEV * TOP)
    onehot = (flat_ids[:, :, None] == jnp.arange(EXPERTS, dtype=jnp.int32)[None, None, :]).astype(jnp.int32)
    counted = jnp.cumsum(onehot, axis=1)
    return jnp.sum(counted * onehot, axis=2).astype(jnp.int32) - 1


def reference(tokens, expert_ids, combine_weights, gate_weight, up_weight, down_weight):
    rank = ranks_of(expert_ids)
    flat_ids = expert_ids.reshape(N_EXPERT, TOK_DEV * TOP)
    source = jnp.arange(N_EXPERT, dtype=jnp.int32)[:, None]
    slot = flat_ids * (N_EXPERT * MOST) + source * MOST + rank
    token_index = source * TOK_DEV + jnp.arange(TOK_DEV * TOP, dtype=jnp.int32)[None, :] // TOP
    table = jnp.full((EXPERTS * N_EXPERT * MOST,), TOKENS, jnp.int32)
    table = table.at[slot.reshape(-1)].set(token_index.reshape(-1))
    padded = jnp.concatenate([tokens, jnp.zeros((1, D), jnp.bfloat16)], axis=0)
    group = FF // N_WIDTH

    def one_expert(packed):
        gate_one, up_one, down_one, rows_index = packed
        rows = padded[rows_index]
        total = jnp.zeros((rows.shape[0], D), jnp.float32)
        for index in range(N_WIDTH):
            gate = jnp.dot(rows, gate_one[:, index * group:(index + 1) * group], preferred_element_type=jnp.float32)
            up = jnp.dot(rows, up_one[:, index * group:(index + 1) * group], preferred_element_type=jnp.float32)
            hidden = (jax.nn.silu(gate) * up).astype(jnp.bfloat16)
            partial_value = jnp.dot(hidden, down_one[index * group:(index + 1) * group, :], preferred_element_type=jnp.float32)
            total = total + partial_value.astype(jnp.bfloat16).astype(jnp.float32)
        return total

    outputs = lax.map(one_expert, (gate_weight, up_weight, down_weight, table.reshape(EXPERTS, N_EXPERT * MOST)))
    outputs = outputs.reshape(EXPERTS * N_EXPERT * MOST, D)
    slot_tokens = slot.reshape(TOKENS, TOP)
    mixed = jnp.zeros((TOKENS, D), jnp.float32)
    for choice_index in range(TOP):
        mixed = mixed + combine_weights[:, choice_index:choice_index + 1] * outputs[slot_tokens[:, choice_index]]
    return mixed.astype(jnp.bfloat16)
```

```python
import jax
import jax.numpy as jnp
from jax import lax
from jax.sharding import PartitionSpec as P


def local(tokens, expert_ids, combine_weights, gate_weight, up_weight, down_weight):
    rows, width_all = tokens.shape
    exp_local, _, ff = gate_weight.shape
    n_expert = lax.axis_size("expert")
    n_width = lax.axis_size("width")
    experts_all = exp_local * n_expert
    cols = width_all // n_width
    part = rows // n_width
    named = expert_ids[:, :, None] == jnp.arange(experts_all, dtype=jnp.int32)
    dense = jnp.sum(jnp.where(named, combine_weights[:, :, None], 0.0), axis=1)
    dense = lax.all_gather(dense, "expert", axis=0, tiled=True)
    dense = lax.dynamic_slice_in_dim(dense, lax.axis_index("expert") * exp_local, exp_local, 1)
    own = lax.dynamic_slice_in_dim(tokens, lax.axis_index("width") * part, part, 0)
    every = lax.all_gather(own, ("expert", "width"), axis=0, tiled=True)
    gate = jnp.einsum("td,kdf->ktf", every, gate_weight, preferred_element_type=jnp.float32)
    up_part = jnp.einsum("td,kdf->ktf", every, up_weight, preferred_element_type=jnp.float32)
    hidden = (jax.nn.silu(gate) * up_part * dense.T[:, :, None]).astype(jnp.bfloat16)
    partial_value = jnp.einsum(
        "ktf,kfd->td", hidden, down_weight, preferred_element_type=jnp.float32
    ).astype(jnp.bfloat16)
    blocks = partial_value.reshape(n_expert, rows, n_width, cols).transpose(0, 2, 1, 3)
    blocks = blocks.reshape(n_expert * n_width * rows, cols)
    return lax.psum_scatter(blocks, ("expert", "width"), scatter_dimension=0, tiled=True)


def solution(mesh):
    placed = (
        P("expert", None),
        P("expert", None),
        P("expert", None),
        P("expert", None, "width"),
        P("expert", None, "width"),
        P("expert", "width", None),
    )
    return jax.shard_map(
        local, mesh=mesh, in_specs=placed, out_specs=P("expert", "width"), check_vma=False
    )
```

```python
import functools

import jax
import jax.numpy as jnp
from jax import lax
from jax.experimental import pallas as pl
from jax.experimental.pallas import tpu as pltpu
from jax.sharding import PartitionSpec as P

LANE = 128
F32 = jnp.float32


def kernel(nz, shared, single, exp_local, rows, width_all, ff,
           x_ref, g_hbm, u_hbm, d_hbm, out_ref, land,
           gw, uw, dw, xbuf, acc, hid, part, r1, ys, xs, yr2, xr2, x3s, y3s, x3r, y3r,
           zsb, zr4, wsem, lsem, zs, zr, xsnd, xr, ysnd, yr, csnd, cr,
           s1s, s1r, s2s, s2r, s3s, s3r, s4s, s4r):
    e, w = lax.axis_index("expert"), lax.axis_index("width")
    z, x = e // 2, e % 2
    y, c = w // 2, w % 2
    cols = width_all // 4
    half = cols // 2
    xdev = (z * 2 + 1 - x, w)
    ydev = (e, (1 - y) * 2 + c)
    cdev = (e, y * 2 + 1 - c)

    def zdev(q):
        return ((z + q) % nz) * 2 + x, w

    weights = [
        pltpu.make_async_copy(src, dst, wsem.at[i])
        for i, (src, dst) in enumerate(((g_hbm, gw), (u_hbm, uw), (d_hbm, dw)))
    ]
    for copy in weights:
        copy.start()

    barrier = pltpu.get_barrier_semaphore()
    peers = [zdev(q) for q in range(1, nz)] + [xdev, ydev, cdev]
    for peer in peers:
        pl.semaphore_signal(barrier, inc=1, device_id=peer, device_id_type=pl.DeviceIdType.MESH)
    pl.semaphore_wait(barrier, len(peers))

    def remote(src, dst, send, recv, dev):
        return pltpu.make_async_remote_copy(
            src_ref=src, dst_ref=dst, send_sem=send, recv_sem=recv,
            device_id=dev, device_id_type=pl.DeviceIdType.MESH)

    sends = []

    def go(copy):
        copy.start()
        sends.append(copy)

    def span(kind, owner):
        if kind == 0:
            return pl.ds(pl.multiple_of(owner * shared, LANE), shared)
        return pl.ds(pl.multiple_of(4 * shared + owner * single, LANE), single)

    own_span = (span(0, w), span(1, c))
    y_span = span(0, (1 - y) * 2 + c)

    def block(p, j):
        return ((z + p) % nz) * 2 + (x if j == 0 else 1 - x)

    def source(p, j, cut):
        if p == 0 and j == 0:
            return x_ref.at[:, cut]
        return land.at[block(p, j), :, cut]

    def send_own():
        for i in range(2):
            go(remote(x_ref.at[:, own_span[i]], land.at[e, :, own_span[i]],
                      xsnd.at[0, i], xr.at[0, i], xdev))
        for q in range(1, nz):
            for i in range(2):
                go(remote(x_ref.at[:, own_span[i]], land.at[e, :, own_span[i]],
                          zs.at[q, i], zr.at[nz - q, i], zdev(q)))

    def spread(p, j):
        ref = land.at[block(p, j), :, own_span[0]]
        go(remote(ref, ref, ysnd.at[p, j], yr.at[p, j], ydev))
        for i in range(2):
            ref = land.at[block(p, j), :, own_span[i]]
            go(remote(ref, ref, csnd.at[p, j, i], cr.at[p, j, i], cdev))

    def take_z(p):
        for i in range(2):
            ref = land.at[block(p, 0), :, own_span[i]]
            remote(ref, ref, zs.at[0, i], zr.at[p, i], xdev).wait_recv()
            go(remote(ref, ref, xsnd.at[p, i], xr.at[p, i], xdev))
        spread(p, 0)

    def take_x(p):
        for i in range(2):
            ref = land.at[block(p, 1), :, own_span[i]]
            remote(ref, ref, zs.at[0, i], xr.at[p, i], xdev).wait_recv()
        spread(p, 1)

    def blocks_of(p):
        return (1,) if p == 0 else (0, 1)

    def take_y(p):
        for j in blocks_of(p):
            ref = land.at[block(p, j), :, y_span]
            remote(ref, ref, zs.at[0, 0], yr.at[p, j], ydev).wait_recv()
            go(remote(ref, ref, csnd.at[p, j, 2], cr.at[p, j, 2], cdev))

    def take_c(p):
        other = (span(0, y * 2 + 1 - c), span(1, 1 - c), span(0, (1 - y) * 2 + 1 - c))
        for j in blocks_of(p):
            for i in range(3):
                ref = land.at[block(p, j), :, other[i]]
                remote(ref, ref, zs.at[0, 0], cr.at[p, j, i], cdev).wait_recv()
        for j in blocks_of(p):
            pltpu.make_async_copy(land.at[block(p, j)], xbuf.at[p % 2, j], lsem.at[j]).start()

    def load_wait(p):
        for j in blocks_of(p):
            pltpu.make_async_copy(land.at[block(p, j)], xbuf.at[p % 2, j], lsem.at[j]).wait()

    def mine(yy):
        return pl.multiple_of((2 * (y if yy == 0 else 1 - y) + c) * cols, LANE)

    stage1, stage2, stage3, stage4 = {}, {}, {}, {}

    def send1(p):
        stage1[p] = []
        for yy in range(2):
            begin = pl.multiple_of((2 * (y if yy == 0 else 1 - y) + 1 - c) * cols, LANE)
            copy = remote(part.at[p % 2, :, :, pl.ds(begin, cols)], r1.at[p, yy],
                          s1s.at[p, yy], s1r.at[p, yy], cdev)
            copy.start()
            stage1[p].append(copy)

    def sum1(p, yy, jj, begin):
        return (part[p % 2, jj, :, pl.ds(pl.multiple_of(mine(yy) + begin, LANE), half)].astype(F32)
                + r1[p, yy, jj, :, pl.ds(begin, half)].astype(F32))

    def do1(p):
        for copy in stage1[p]:
            copy.wait()
        s = p % 2
        if p >= 2:
            for copy in stage2[p - 2]:
                copy.wait_send()
        for i in range(2):
            ys[s, i] = sum1(p, 1, i, 0).astype(jnp.bfloat16)
            xs[s, i] = sum1(p, i, 1, half).astype(jnp.bfloat16)
        stage2[p] = [remote(ys.at[s], yr2.at[p], s2s.at[p, 0], s2r.at[p, 0], ydev),
                     remote(xs.at[s], xr2.at[p], s2s.at[p, 1], s2r.at[p, 1], xdev)]
        for copy in stage2[p]:
            copy.start()

    def do2(p):
        for copy in stage2[p]:
            copy.wait_recv()
        s = p % 2
        if p >= 2:
            for copy in stage3[p - 2]:
                copy.wait_send()
        x3s[s] = (sum1(p, 0, 1, 0) + yr2[p, 1].astype(F32)).astype(jnp.bfloat16)
        y3s[s] = (sum1(p, 1, 0, half) + xr2[p, 1].astype(F32)).astype(jnp.bfloat16)
        stage3[p] = [remote(x3s.at[s], x3r.at[p], s3s.at[p, 0], s3r.at[p, 0], xdev),
                     remote(y3s.at[s], y3r.at[p], s3s.at[p, 1], s3r.at[p, 1], ydev)]
        for copy in stage3[p]:
            copy.start()

    def do3(p):
        for copy in stage3[p]:
            copy.wait_recv()
        s = p % 2
        left = sum1(p, 0, 0, 0) + yr2[p, 0].astype(F32) + x3r[p].astype(F32)
        right = sum1(p, 0, 0, half) + xr2[p, 0].astype(F32) + y3r[p].astype(F32)
        if p >= 3:
            stage4[p - 2].wait_send()
        if p == 0:
            zr4[0, :, 0:half] = left.astype(jnp.bfloat16)
            zr4[0, :, half:cols] = right.astype(jnp.bfloat16)
        else:
            zsb[s, :, 0:half] = left.astype(jnp.bfloat16)
            zsb[s, :, half:cols] = right.astype(jnp.bfloat16)
            stage4[p] = remote(zsb.at[s], zr4.at[nz - p], s4s.at[p], s4r.at[nz - p], zdev(p))
            stage4[p].start()

    def up(p, k):
        s = p % 2
        dense = xbuf[s, :, :, width_all:].reshape(2 * rows, -1).astype(F32)
        lane = lax.broadcasted_iota(jnp.int32, dense.shape, 1)
        scale = jnp.sum(jnp.where(lane == e * exp_local + k, dense, 0.0), axis=1, keepdims=True)
        deep = 1024
        acc[...] = jnp.zeros_like(acc)

        @pl.loop(0, width_all // deep)
        def _(i):
            at = pl.ds(pl.multiple_of(i * deep, LANE), deep)
            xa = xbuf[s, :, :, at].reshape(2 * rows, deep)
            acc[0] += jnp.dot(xa, gw[k, at, :], preferred_element_type=F32)
            acc[1] += jnp.dot(xa, uw[k, at, :], preferred_element_type=F32)

        gate, upp = acc[0], acc[1]
        hid[:, k * ff:(k + 1) * ff] = (jax.nn.silu(gate) * upp * scale).astype(jnp.bfloat16)

    def down(p, piece, pieces):
        tile = 512
        count = width_all // tile // pieces

        @pl.loop(0, count)
        def _(i):
            at = pl.ds(pl.multiple_of((piece * count + i) * tile, LANE), tile)
            value = jnp.dot(hid[...], dw[:, at], preferred_element_type=F32)
            part[p % 2, :, :, at] = value.astype(jnp.bfloat16).reshape(2, rows, tile)

    send_own()
    own_load = pltpu.make_async_copy(x_ref, xbuf.at[0, 0], lsem.at[2])
    own_load.start()
    take_x(0)
    if nz > 1:
        take_z(1)
    take_y(0)
    take_c(0)
    own_load.wait()
    for copy in weights:
        copy.wait()
    for p in range(nz):
        load_wait(p)
        up(p, 0)
        if p + 2 < nz:
            take_z(p + 2)
        if p >= 1:
            do1(p - 1)
        for k in range(1, exp_local):
            up(p, k)
        if p + 1 < nz:
            take_x(p + 1)
        if p >= 1:
            do2(p - 1)
        down(p, 0, 2)
        if p + 1 < nz:
            take_y(p + 1)
        if p >= 1:
            do3(p - 1)
        down(p, 1, 2)
        send1(p)
        if p + 1 < nz:
            take_c(p + 1)
    do1(nz - 1)
    do2(nz - 1)
    do3(nz - 1)
    total = zr4[0].astype(F32)
    for p in range(1, nz):
        remote(zr4.at[p], zr4.at[p], s4s.at[0], s4r.at[p], xdev).wait_recv()
        total = total + zr4[p].astype(F32)
    out_ref[...] = total.astype(jnp.bfloat16)
    for copy in sends:
        copy.wait_send()
    for p in range(max(0, nz - 2), nz):
        for copy in stage2[p] + stage3[p]:
            copy.wait_send()
    for p in range(max(1, nz - 2), nz):
        stage4[p].wait_send()


def local(tokens, expert_ids, combine_weights, gate_weight, up_weight, down_weight):
    rows, width_all = tokens.shape
    exp_local, _, ff = gate_weight.shape
    n_expert = lax.axis_size("expert")
    n_width = lax.axis_size("width")
    assert n_width == 4 and n_expert % 2 == 0
    nz = n_expert // 2
    experts_all = exp_local * n_expert
    lanes = -(-experts_all // (2 * LANE)) * 2 * LANE
    cols = width_all // n_width
    tiles = (width_all + lanes) // LANE
    shared = tiles * 5 // 34
    if (tiles - 4 * shared) % 2:
        raise ValueError("tiles")
    single = (tiles - 4 * shared) // 2 * LANE
    shared = shared * LANE
    named = expert_ids[:, :, None] == jnp.arange(lanes, dtype=jnp.int32)
    dense = jnp.sum(jnp.where(named, combine_weights[:, :, None], 0.0), axis=1)
    wide = jnp.concatenate([tokens, dense.astype(jnp.bfloat16)], axis=1)
    total = width_all + lanes
    half = cols // 2
    bf = jnp.bfloat16
    dma = pltpu.SemaphoreType.DMA
    anyspace = pl.BlockSpec(memory_space=pl.ANY)
    out, _ = pl.pallas_call(
        functools.partial(kernel, nz, shared, single, exp_local, rows, width_all, ff),
        out_shape=(jax.ShapeDtypeStruct((rows, cols), bf),
                   jax.ShapeDtypeStruct((n_expert, rows, total), bf)),
        in_specs=[anyspace] * 4,
        out_specs=(pl.BlockSpec(memory_space=pltpu.VMEM), anyspace),
        scratch_shapes=[
            pltpu.VMEM(gate_weight.shape, bf),
            pltpu.VMEM(up_weight.shape, bf),
            pltpu.VMEM((exp_local * ff, width_all), bf),
            pltpu.VMEM((2, 2, rows, total), bf),
            pltpu.VMEM((2, 2 * rows, ff), F32),
            pltpu.VMEM((2 * rows, exp_local * ff), bf),
            pltpu.VMEM((2, 2, rows, width_all), bf),
            pltpu.VMEM((nz, 2, 2, rows, cols), bf),
            pltpu.VMEM((2, 2, rows, half), bf),
            pltpu.VMEM((2, 2, rows, half), bf),
            pltpu.VMEM((nz, 2, rows, half), bf),
            pltpu.VMEM((nz, 2, rows, half), bf),
            pltpu.VMEM((2, rows, half), bf),
            pltpu.VMEM((2, rows, half), bf),
            pltpu.VMEM((nz, rows, half), bf),
            pltpu.VMEM((nz, rows, half), bf),
            pltpu.VMEM((2, rows, cols), bf),
            pltpu.VMEM((nz, rows, cols), bf),
            dma((3,)), dma((3,)),
            dma((nz, 2)), dma((nz, 2)), dma((nz, 2)), dma((nz, 2)),
            dma((nz, 2)), dma((nz, 2)), dma((nz, 2, 3)), dma((nz, 2, 3)),
            dma((nz, 2)), dma((nz, 2)), dma((nz, 2)), dma((nz, 2)),
            dma((nz, 2)), dma((nz, 2)), dma((nz,)), dma((nz,)),
        ],
        compiler_params=pltpu.CompilerParams(
            collective_id=0, has_side_effects=True, vmem_limit_bytes=67_043_328),
    )(wide, gate_weight, up_weight, down_weight.reshape(exp_local * ff, width_all))
    return out


def solution(mesh):
    placed = (
        P("expert", None),
        P("expert", None),
        P("expert", None),
        P("expert", None, "width"),
        P("expert", None, "width"),
        P("expert", "width", None),
    )
    return jax.shard_map(
        local, mesh=mesh, in_specs=placed, out_specs=P("expert", "width"), check_vma=False
    )
```

```python
import functools

import jax
import jax.numpy as jnp
from jax import lax
from jax.experimental import pallas as pl
from jax.experimental.pallas import tpu as pltpu
from jax.sharding import PartitionSpec as P

LANE = 128
F32 = jnp.float32


def kernel(nz, shared, single, exp_local, rows, width_all, ff,
           x_ref, g_hbm, u_hbm, d_hbm, out_ref, land,
           gw, uw, dw, xbuf, acc, hid, part, r1, ys, xs, yr2, xr2, x3s, y3s, x3r, y3r,
           zsb, zr4, wsem, lsem, zs, zr, xsnd, xr, ysnd, yr, csnd, cr,
           s1s, s1r, s2s, s2r, s3s, s3r, s4s, s4r):
    e, w = lax.axis_index("expert"), lax.axis_index("width")
    z, x = e // 2, e % 2
    y, c = w // 2, w % 2
    cols = width_all // 4
    half = cols // 2
    xdev = (z * 2 + 1 - x, w)
    ydev = (e, (1 - y) * 2 + c)
    cdev = (e, y * 2 + 1 - c)

    def zdev(q):
        return ((z + q) % nz) * 2 + x, w

    weights = [
        pltpu.make_async_copy(src, dst, wsem.at[i])
        for i, (src, dst) in enumerate(((g_hbm, gw), (u_hbm, uw), (d_hbm, dw)))
    ]
    for copy in weights:
        copy.start()

    barrier = pltpu.get_barrier_semaphore()
    peers = [zdev(q) for q in range(1, nz)] + [xdev, ydev, cdev]
    for peer in peers:
        pl.semaphore_signal(barrier, inc=1, device_id=peer, device_id_type=pl.DeviceIdType.MESH)
    pl.semaphore_wait(barrier, len(peers))

    def remote(src, dst, send, recv, dev):
        return pltpu.make_async_remote_copy(
            src_ref=src, dst_ref=dst, send_sem=send, recv_sem=recv,
            device_id=dev, device_id_type=pl.DeviceIdType.MESH)

    sends = []

    def go(copy):
        copy.start()
        sends.append(copy)

    def span(kind, owner):
        if kind == 0:
            return pl.ds(pl.multiple_of(owner * shared, LANE), shared)
        return pl.ds(pl.multiple_of(4 * shared + owner * single, LANE), single)

    own_span = (span(0, w), span(1, c))
    y_span = span(0, (1 - y) * 2 + c)

    def block(p, j):
        return ((z + p) % nz) * 2 + (x if j == 0 else 1 - x)

    def source(p, j, cut):
        if p == 0 and j == 0:
            return x_ref.at[:, cut]
        return land.at[block(p, j), :, cut]

    def send_own():
        for i in range(2):
            go(remote(x_ref.at[:, own_span[i]], land.at[e, :, own_span[i]],
                      xsnd.at[0, i], xr.at[0, i], xdev))
        for q in range(1, nz):
            for i in range(2):
                go(remote(x_ref.at[:, own_span[i]], land.at[e, :, own_span[i]],
                          zs.at[q, i], zr.at[nz - q, i], zdev(q)))

    def spread(p, j):
        ref = land.at[block(p, j), :, own_span[0]]
        go(remote(ref, ref, ysnd.at[p, j], yr.at[p, j], ydev))
        for i in range(2):
            ref = land.at[block(p, j), :, own_span[i]]
            go(remote(ref, ref, csnd.at[p, j, i], cr.at[p, j, i], cdev))

    def take_z(p):
        for i in range(2):
            ref = land.at[block(p, 0), :, own_span[i]]
            remote(ref, ref, zs.at[0, i], zr.at[p, i], xdev).wait_recv()
            go(remote(ref, ref, xsnd.at[p, i], xr.at[p, i], xdev))
        spread(p, 0)

    def take_x(p):
        for i in range(2):
            ref = land.at[block(p, 1), :, own_span[i]]
            remote(ref, ref, zs.at[0, i], xr.at[p, i], xdev).wait_recv()
        spread(p, 1)

    def blocks_of(p):
        return (1,) if p == 0 else (0, 1)

    def take_y(p):
        for j in blocks_of(p):
            ref = land.at[block(p, j), :, y_span]
            remote(ref, ref, zs.at[0, 0], yr.at[p, j], ydev).wait_recv()
            go(remote(ref, ref, csnd.at[p, j, 2], cr.at[p, j, 2], cdev))

    def take_c(p):
        other = (span(0, y * 2 + 1 - c), span(1, 1 - c), span(0, (1 - y) * 2 + 1 - c))
        for j in blocks_of(p):
            for i in range(3):
                ref = land.at[block(p, j), :, other[i]]
                remote(ref, ref, zs.at[0, 0], cr.at[p, j, i], cdev).wait_recv()
        for j in blocks_of(p):
            pltpu.make_async_copy(land.at[block(p, j)], xbuf.at[p % 2, j], lsem.at[j]).start()

    def load_wait(p):
        for j in blocks_of(p):
            pltpu.make_async_copy(land.at[block(p, j)], xbuf.at[p % 2, j], lsem.at[j]).wait()

    def mine(yy):
        return pl.multiple_of((2 * (y if yy == 0 else 1 - y) + c) * cols, LANE)

    stage1, stage2, stage3, stage4 = {}, {}, {}, {}

    def send1(p):
        stage1[p] = []
        for yy in range(2):
            begin = pl.multiple_of((2 * (y if yy == 0 else 1 - y) + 1 - c) * cols, LANE)
            copy = remote(part.at[p % 2, :, :, pl.ds(begin, cols)], r1.at[p, yy],
                          s1s.at[p, yy], s1r.at[p, yy], cdev)
            copy.start()
            stage1[p].append(copy)

    def sum1(p, yy, jj, begin):
        return (part[p % 2, jj, :, pl.ds(pl.multiple_of(mine(yy) + begin, LANE), half)].astype(F32)
                + r1[p, yy, jj, :, pl.ds(begin, half)].astype(F32))

    def do1(p):
        for copy in stage1[p]:
            copy.wait()
        s = p % 2
        if p >= 2:
            for copy in stage2[p - 2]:
                copy.wait_send()
        for i in range(2):
            ys[s, i] = sum1(p, 1, i, 0).astype(jnp.bfloat16)
            xs[s, i] = sum1(p, i, 1, half).astype(jnp.bfloat16)
        stage2[p] = [remote(ys.at[s], yr2.at[p], s2s.at[p, 0], s2r.at[p, 0], ydev),
                     remote(xs.at[s], xr2.at[p], s2s.at[p, 1], s2r.at[p, 1], xdev)]
        for copy in stage2[p]:
            copy.start()

    def do2(p):
        for copy in stage2[p]:
            copy.wait_recv()
        s = p % 2
        if p >= 2:
            for copy in stage3[p - 2]:
                copy.wait_send()
        x3s[s] = (sum1(p, 0, 1, 0) + yr2[p, 1].astype(F32)).astype(jnp.bfloat16)
        y3s[s] = (sum1(p, 1, 0, half) + xr2[p, 1].astype(F32)).astype(jnp.bfloat16)
        stage3[p] = [remote(x3s.at[s], x3r.at[p], s3s.at[p, 0], s3r.at[p, 0], xdev),
                     remote(y3s.at[s], y3r.at[p], s3s.at[p, 1], s3r.at[p, 1], ydev)]
        for copy in stage3[p]:
            copy.start()

    def do3(p):
        for copy in stage3[p]:
            copy.wait_recv()
        s = p % 2
        left = sum1(p, 0, 0, 0) + yr2[p, 0].astype(F32) + x3r[p].astype(F32)
        right = sum1(p, 0, 0, half) + xr2[p, 0].astype(F32) + y3r[p].astype(F32)
        if p >= 3:
            stage4[p - 2].wait_send()
        if p == 0:
            zr4[0, :, 0:half] = left.astype(jnp.bfloat16)
            zr4[0, :, half:cols] = right.astype(jnp.bfloat16)
        else:
            zsb[s, :, 0:half] = left.astype(jnp.bfloat16)
            zsb[s, :, half:cols] = right.astype(jnp.bfloat16)
            stage4[p] = remote(zsb.at[s], zr4.at[nz - p], s4s.at[p], s4r.at[nz - p], zdev(p))
            stage4[p].start()

    def up(p, k):
        s = p % 2
        dense = xbuf[s, :, :, width_all:].reshape(2 * rows, -1).astype(F32)
        lane = lax.broadcasted_iota(jnp.int32, dense.shape, 1)
        scale = jnp.sum(jnp.where(lane == e * exp_local + k, dense, 0.0), axis=1, keepdims=True)
        deep = 1024
        acc[...] = jnp.zeros_like(acc)

        @pl.loop(0, width_all // deep)
        def _(i):
            at = pl.ds(pl.multiple_of(i * deep, LANE), deep)
            xa = xbuf[s, :, :, at].reshape(2 * rows, deep)
            acc[0] += jnp.dot(xa, gw[k, at, :], preferred_element_type=F32)
            acc[1] += jnp.dot(xa, uw[k, at, :], preferred_element_type=F32)

        gate, upp = acc[0], acc[1]
        hid[:, k * ff:(k + 1) * ff] = (jax.nn.silu(gate) * upp * scale).astype(jnp.bfloat16)

    def down(p, piece, pieces):
        tile = 512
        count = width_all // tile // pieces

        @pl.loop(0, count)
        def _(i):
            at = pl.ds(pl.multiple_of((piece * count + i) * tile, LANE), tile)
            value = jnp.dot(hid[...], dw[:, at], preferred_element_type=F32)
            part[p % 2, :, :, at] = value.astype(jnp.bfloat16).reshape(2, rows, tile)

    send_own()
    own_load = pltpu.make_async_copy(x_ref, xbuf.at[0, 0], lsem.at[2])
    own_load.start()
    take_x(0)
    if nz > 1:
        take_z(1)
    take_y(0)
    take_c(0)
    own_load.wait()
    for copy in weights:
        copy.wait()
    for p in range(nz):
        load_wait(p)
        up(p, 0)
        if p + 2 < nz:
            take_z(p + 2)
        if p >= 2:
            do3(p - 2)
        for k in range(1, exp_local):
            up(p, k)
        if p + 1 < nz:
            take_x(p + 1)
        if p >= 1:
            do1(p - 1)
        down(p, 0, 2)
        if p + 1 < nz:
            take_y(p + 1)
        down(p, 1, 2)
        send1(p)
        if p + 1 < nz:
            take_c(p + 1)
        if p >= 1:
            do2(p - 1)
    do1(nz - 1)
    if nz >= 2:
        do3(nz - 2)
    do2(nz - 1)
    do3(nz - 1)
    total = zr4[0].astype(F32)
    for p in range(1, nz):
        remote(zr4.at[p], zr4.at[p], s4s.at[0], s4r.at[p], xdev).wait_recv()
        total = total + zr4[p].astype(F32)
    out_ref[...] = total.astype(jnp.bfloat16)
    for copy in sends:
        copy.wait_send()
    for p in range(max(0, nz - 2), nz):
        for copy in stage2[p] + stage3[p]:
            copy.wait_send()
    for p in range(max(1, nz - 2), nz):
        stage4[p].wait_send()


def local(tokens, expert_ids, combine_weights, gate_weight, up_weight, down_weight):
    rows, width_all = tokens.shape
    exp_local, _, ff = gate_weight.shape
    n_expert = lax.axis_size("expert")
    n_width = lax.axis_size("width")
    assert n_width == 4 and n_expert % 2 == 0
    nz = n_expert // 2
    experts_all = exp_local * n_expert
    lanes = -(-experts_all // (2 * LANE)) * 2 * LANE
    cols = width_all // n_width
    tiles = (width_all + lanes) // LANE
    shared = tiles * 5 // 34
    if (tiles - 4 * shared) % 2:
        raise ValueError("tiles")
    single = (tiles - 4 * shared) // 2 * LANE
    shared = shared * LANE
    named = expert_ids[:, :, None] == jnp.arange(lanes, dtype=jnp.int32)
    dense = jnp.sum(jnp.where(named, combine_weights[:, :, None], 0.0), axis=1)
    wide = jnp.concatenate([tokens, dense.astype(jnp.bfloat16)], axis=1)
    total = width_all + lanes
    half = cols // 2
    bf = jnp.bfloat16
    dma = pltpu.SemaphoreType.DMA
    anyspace = pl.BlockSpec(memory_space=pl.ANY)
    out, _ = pl.pallas_call(
        functools.partial(kernel, nz, shared, single, exp_local, rows, width_all, ff),
        out_shape=(jax.ShapeDtypeStruct((rows, cols), bf),
                   jax.ShapeDtypeStruct((n_expert, rows, total), bf)),
        in_specs=[anyspace] * 4,
        out_specs=(pl.BlockSpec(memory_space=pltpu.VMEM), anyspace),
        scratch_shapes=[
            pltpu.VMEM(gate_weight.shape, bf),
            pltpu.VMEM(up_weight.shape, bf),
            pltpu.VMEM((exp_local * ff, width_all), bf),
            pltpu.VMEM((2, 2, rows, total), bf),
            pltpu.VMEM((2, 2 * rows, ff), F32),
            pltpu.VMEM((2 * rows, exp_local * ff), bf),
            pltpu.VMEM((2, 2, rows, width_all), bf),
            pltpu.VMEM((nz, 2, 2, rows, cols), bf),
            pltpu.VMEM((2, 2, rows, half), bf),
            pltpu.VMEM((2, 2, rows, half), bf),
            pltpu.VMEM((nz, 2, rows, half), bf),
            pltpu.VMEM((nz, 2, rows, half), bf),
            pltpu.VMEM((2, rows, half), bf),
            pltpu.VMEM((2, rows, half), bf),
            pltpu.VMEM((nz, rows, half), bf),
            pltpu.VMEM((nz, rows, half), bf),
            pltpu.VMEM((2, rows, cols), bf),
            pltpu.VMEM((nz, rows, cols), bf),
            dma((3,)), dma((3,)),
            dma((nz, 2)), dma((nz, 2)), dma((nz, 2)), dma((nz, 2)),
            dma((nz, 2)), dma((nz, 2)), dma((nz, 2, 3)), dma((nz, 2, 3)),
            dma((nz, 2)), dma((nz, 2)), dma((nz, 2)), dma((nz, 2)),
            dma((nz, 2)), dma((nz, 2)), dma((nz,)), dma((nz,)),
        ],
        compiler_params=pltpu.CompilerParams(
            collective_id=0, has_side_effects=True, vmem_limit_bytes=67_043_328),
    )(wide, gate_weight, up_weight, down_weight.reshape(exp_local * ff, width_all))
    return out


def solution(mesh):
    placed = (
        P("expert", None),
        P("expert", None),
        P("expert", None),
        P("expert", None, "width"),
        P("expert", None, "width"),
        P("expert", "width", None),
    )
    return jax.shard_map(
        local, mesh=mesh, in_specs=placed, out_specs=P("expert", "width"), check_vma=False
    )
```
